32 devices in a mesh: seq: 16 (over z, y, x), head: 2 (over core).
Axes of the slice: x: 2, y: 2, z: 4, core: 2. Of those that a mesh axis runs over, the one named last changes fastest.
Arguments:
- queries: bfloat16 [8192, 2048], P('seq', 'head'), may hold values from -37.123106012293746 to 37.123106012293746
- keys: bfloat16 [8192, 2048], P('seq', 'head'), may hold values from -6 to 6
- values: bfloat16 [8192, 2048], P('seq', 'head'), may hold values from -24 to 24
- rand_blocks: int32 [128, 16], P('seq', 'head'), may hold values from 0 to 127, as said below
- global_blocks: int32 [2], replicated, may hold values from 0 to 127
- out_weight: bfloat16 [2048, 4096], P(('head', 'seq')), may hold values from -0.125 to 0.125
Outputs:
- layer_out: bfloat16 [8192, 4096], P(('seq', 'head'))
The draws below stay inside these ranges and needn't reach their ends.
Inputs may be any that keep to these rules, and one draw needn't show every extreme that they name: `rand_blocks`: of the 8 x 8 entries of one device, at most 8 name blocks of one and the same index of seq (block id // 8), and some index of seq is named exactly 8 times by them.
All inputs are finite; a program needn't handle non-finite values.
Results may differ from the reference program's by a relative error of at most 0.013.
Values may be sent and summed in bfloat16 or wider, within the bound.
A program may use at most 128 MiB of HBM per device.

```python
import jax
import jax.numpy as jnp
from jax import lax

D = 4096
H = 16
DH = 128
BLK = 64
G = 2
QB_DEV = 8
HG = 8
NQB = 128
TOKENS = 8192
CAP = 8
N_SEQ = 16
N_HEAD = 2


def draw_queries(key, part):
    drawn = jax.random.truncated_normal(jax.random.fold_in(key, 1), -6.0, 6.0, (TOKENS, H * DH), jnp.float32)
    return drawn.astype(jnp.bfloat16)


def draw_keys(key, part):
    drawn = jax.random.truncated_normal(jax.random.fold_in(key, 2), -6.0, 6.0, (TOKENS, H * DH), jnp.float32)
    return drawn.astype(jnp.bfloat16)


def draw_rand_blocks(key, part):
    total = QB_DEV * HG

    def single(subkey):
        key_first, key_rest, key_order, key_local = jax.random.split(subkey, 4)
        first = jax.random.randint(key_first, (), 0, N_SEQ)
        rest = jax.random.permutation(key_rest, N_SEQ * CAP - CAP)[:total - CAP] + CAP
        slots = jnp.concatenate([jnp.arange(CAP, dtype=jnp.int32), rest.astype(jnp.int32)])
        owners = (slots // CAP + first) % N_SEQ
        owners = jax.random.permutation(key_order, owners)
        local = jax.random.randint(key_local, (total,), 0, QB_DEV)
        return (owners * QB_DEV + local).astype(jnp.int32)
    subkeys = jax.random.split(jax.random.fold_in(key, 11), N_SEQ * N_HEAD)
    ids = jax.vmap(single)(subkeys).reshape(N_SEQ, N_HEAD, QB_DEV, HG)
    return ids.transpose(0, 2, 1, 3).reshape(NQB, H)


def level_of(own_key, extent, shards, least, top_value):
    factor_of, own = 1.0, jax.random.fold_in(own_key, 6)
    for position, blocks in shards:
        heights = jnp.exp(jax.random.uniform(jax.random.fold_in(own, position), (blocks,), jnp.float32, least / len(shards), top_value / len(shards)))
        factor_of = factor_of * jnp.repeat(heights, extent[position] // blocks).reshape([-1 if axis == position else 1 for axis in range(len(extent))])
    return factor_of


def normal_values(key, shape, scale, limit, cuts=(), kind=jnp.bfloat16):
    values = jax.random.normal(key, shape, jnp.float32) * scale
    if len(cuts) > 0:
        values = level_of(key, shape, cuts, -0.22, 0.18) * values
    return jnp.clip(values, min=-limit, max=limit).astype(kind)


def setup_inputs(seed: int = 0) -> dict:
    splits = jax.random.split(jax.random.key(seed), 7)
    return {
        "queries": draw_queries(jax.random.fold_in(splits[6], 71), 0),
        "keys": draw_keys(jax.random.fold_in(splits[6], 71), 0),
        "values": normal_values(splits[2], (TOKENS, H * DH), 4.0, 24.0, ((0, 16), (1, 2))),
        "rand_blocks": draw_rand_blocks(jax.random.fold_in(splits[6], 71), 0),
        "global_blocks": jax.random.randint(splits[4], (G,), 0, NQB).astype(jnp.int32),
        "out_weight": normal_values(splits[5], (H * DH, D), (H * DH) ** -0.5, 0.125, ((0, 32),)),
    }


def reference(queries, keys, values, rand_blocks, global_blocks, out_weight):
    f32 = jnp.float32
    query_blocks = queries.reshape(NQB, BLK, H, DH)
    key_blocks = keys.reshape(NQB, BLK, H, DH)
    value_blocks = values.reshape(NQB, BLK, H, DH)
    key_padded = jnp.concatenate([key_blocks[-1:], key_blocks, key_blocks[:1]], axis=0)
    value_padded = jnp.concatenate([value_blocks[-1:], value_blocks, value_blocks[:1]], axis=0)
    global_keys = key_blocks[global_blocks].reshape(G * BLK, H, DH).astype(f32)
    global_values = value_blocks[global_blocks].reshape(G * BLK, H, DH).astype(f32)
    head_iota = jnp.arange(H, dtype=jnp.int32)[None, :]
    group_width = H * DH // N_HEAD
    scale = DH ** -0.5

    def window_of(padded, start):
        beside_all = lax.dynamic_slice_in_dim(padded, start, QB_DEV + 2, 0)
        return jnp.concatenate([beside_all[:-2], beside_all[1:-1], beside_all[2:]], axis=1).astype(f32)

    def span(index):
        start = (index * QB_DEV).astype(jnp.int32)
        query_part = lax.dynamic_slice_in_dim(query_blocks, start, QB_DEV, 0).astype(f32)
        window_keys = window_of(key_padded, start)
        window_values = window_of(value_padded, start)
        chosen_ids = lax.dynamic_slice_in_dim(rand_blocks, start, QB_DEV, 0)
        random_keys = key_blocks[chosen_ids, :, head_iota, :].astype(f32)
        random_values = value_blocks[chosen_ids, :, head_iota, :].astype(f32)
        s_window = jnp.einsum("qbhd,qkhd->qhbk", query_part, window_keys)
        s_global = jnp.einsum("qbhd,khd->qhbk", query_part, global_keys)
        s_random = jnp.einsum("qbhd,qhkd->qhbk", query_part, random_keys)
        scores = jnp.concatenate([s_window, s_global, s_random], axis=-1) * scale
        top = jnp.max(scores, axis=-1, keepdims=True)
        expo = jnp.exp(scores - top)
        weights = (expo / jnp.sum(expo, axis=-1, keepdims=True)).astype(jnp.bfloat16).astype(f32)
        wlen = 3 * BLK
        glen = G * BLK
        context = jnp.einsum("qhbk,qkhd->qbhd", weights[..., :wlen], window_values)
        context = context + jnp.einsum("qhbk,khd->qbhd", weights[..., wlen:wlen + glen], global_values)
        context = context + jnp.einsum("qhbk,qhkd->qbhd", weights[..., wlen + glen:], random_values)
        attended = context.reshape(QB_DEV * BLK, H * DH).astype(jnp.bfloat16)
        summed = jnp.zeros((QB_DEV * BLK, D), f32)
        for group in range(N_HEAD):
            part = jnp.dot(attended[:, group * group_width:(group + 1) * group_width],
                           out_weight[group * group_width:(group + 1) * group_width],
                           preferred_element_type=f32).astype(jnp.bfloat16)
            part = lax.optimization_barrier(part)
            summed = summed + part.astype(f32)
        return summed.astype(jnp.bfloat16)

    result = lax.map(span, jnp.arange(N_SEQ, dtype=jnp.int32))
    return result.reshape(TOKENS, D)
```

```python
import functools

import jax
import jax.numpy as jnp
from jax import lax
from jax.experimental import pallas as pl
from jax.experimental.pallas import tpu as pltpu
from jax.sharding import PartitionSpec as P


def ranked(owners):
    count = owners.shape[0]
    order = jnp.arange(count, dtype=jnp.int32)
    earlier = (owners[:, None] == owners[None, :]) & (order[None, :] < order[:, None])
    return jnp.sum(earlier.astype(jnp.int32), axis=1)


def pack_kernel(cap, block_len, head_dim, head_count, codes_ref, k_ref, v_ref, g_ref, o_ref):
    dst = pl.program_id(0)
    for s in range(cap):
        code = codes_ref[dst * cap + s]
        row = pl.multiple_of(code // head_count * block_len, block_len)
        col = pl.multiple_of(code % head_count * head_dim, head_dim)
        rows = pl.ds(s * block_len, block_len)
        o_ref[0, rows, 0:head_dim] = k_ref[pl.ds(row, block_len), pl.ds(col, head_dim)]
        o_ref[0, rows, head_dim : 2 * head_dim] = v_ref[pl.ds(row, block_len), pl.ds(col, head_dim)]
    o_ref[0, cap * block_len :, :] = g_ref[0]


def pack(codes, keys, values, pieces, cap, block_len, head_dim, head_count):
    n, extra, width = pieces.shape
    rows = cap * block_len + extra
    whole = lambda d, c: (0, 0)
    return pl.pallas_call(
        functools.partial(pack_kernel, cap, block_len, head_dim, head_count),
        out_shape=jax.ShapeDtypeStruct((n, rows, width), keys.dtype),
        grid_spec=pltpu.PrefetchScalarGridSpec(
            num_scalar_prefetch=1,
            grid=(n,),
            in_specs=[
                pl.BlockSpec(keys.shape, whole),
                pl.BlockSpec(values.shape, whole),
                pl.BlockSpec((1, extra, width), lambda d, c: (d, 0, 0)),
            ],
            out_specs=pl.BlockSpec((1, rows, width), lambda d, c: (d, 0, 0)),
        ),
        cost_estimate=pl.CostEstimate(
            flops=0, transcendentals=0, bytes_accessed=2 * n * rows * width * 2
        ),
        name="pack",
    )(codes, keys, values, pieces)


def attend_kernel(
    blocks, block_len, head_dim, head_count, scale,
    own_ref, rank_ref, q_ref, k_ref, v_ref, low_ref, high_ref, kg_ref, vg_ref, arr_ref, o_ref,
):
    h = pl.program_id(0)
    kk = jnp.concatenate([low_ref[0], k_ref[...], high_ref[0]], axis=0)
    vv = jnp.concatenate([low_ref[1], v_ref[...], high_ref[1]], axis=0)
    kg, vg = kg_ref[...], vg_ref[...]
    for b in range(blocks):
        e = b * head_count + h
        owner = own_ref[e]
        rows = pl.ds(pl.multiple_of(rank_ref[e] * block_len, block_len), block_len)
        kr = arr_ref[owner, rows, 0:head_dim]
        vr = arr_ref[owner, rows, head_dim : 2 * head_dim]
        lo, hi = b * block_len, (b + 3) * block_len
        ks = jnp.concatenate([kk[lo:hi], kg, kr], axis=0)
        vs = jnp.concatenate([vv[lo:hi], vg, vr], axis=0)
        q = q_ref[lo : lo + block_len, :]
        s = lax.dot_general(
            q, ks, (((1,), (1,)), ((), ())), preferred_element_type=jnp.float32
        ) * scale
        top = jnp.max(s, axis=-1, keepdims=True)
        expo = jnp.exp(s - top)
        total = jnp.sum(expo, axis=-1, keepdims=True)
        w = (expo * (1.0 / total)).astype(jnp.bfloat16)
        o = jnp.dot(w, vs, preferred_element_type=jnp.float32)
        o_ref[lo : lo + block_len, :] = o.astype(o_ref.dtype)


def attend(owners, ranks, q, k, v, low, high, kg, vg, arrived, blocks, block_len, head_dim, head_count):
    tokens, width = q.shape
    col = lambda h, a, b: (0, h)
    edge = pl.BlockSpec((2, block_len, head_dim), lambda h, a, b: (0, 0, h))
    main = pl.BlockSpec((tokens, head_dim), col)
    glob = pl.BlockSpec((kg.shape[0], head_dim), col)
    return pl.pallas_call(
        functools.partial(
            attend_kernel, blocks, block_len, head_dim, head_count, head_dim ** (-0.5)
        ),
        out_shape=jax.ShapeDtypeStruct(q.shape, jnp.bfloat16),
        grid_spec=pltpu.PrefetchScalarGridSpec(
            num_scalar_prefetch=2,
            grid=(head_count,),
            in_specs=[
                main, main, main, edge, edge, glob, glob,
                pl.BlockSpec(arrived.shape, lambda h, a, b: (0, 0, 0)),
            ],
            out_specs=main,
        ),
        cost_estimate=pl.CostEstimate(
            flops=4 * tokens * 6 * block_len * width,
            transcendentals=tokens * 6 * block_len * head_count,
            bytes_accessed=2 * (4 * q.size + arrived.size),
        ),
        name="attend",
    )(owners, ranks, q, k, v, low, high, kg, vg, arrived)


def body(queries, keys, values, rand_blocks, global_blocks, out_weight):
    f32 = jnp.float32
    n = lax.axis_size("seq")
    block_count, head_count = rand_blocks.shape
    tokens, width = queries.shape
    block_len = tokens // block_count
    head_dim = width // head_count
    entries = block_count * head_count
    cap = max(2, (2 * entries + n - 1) // n)
    g = global_blocks.shape[0]
    wide = 2 * head_dim

    group_rows = lax.all_gather(out_weight, "seq", axis=0, tiled=True)

    flat_blocks = rand_blocks.reshape(entries)
    owners = flat_blocks // block_count
    head_iota = jnp.arange(entries, dtype=jnp.int32) % head_count
    codes = flat_blocks % block_count * head_count + head_iota
    ranks = ranked(owners)
    slots = owners * cap + ranks
    hits = slots[:, None] == jnp.arange(n * cap, dtype=jnp.int32)[None, :]
    outgoing = jnp.sum(jnp.where(hits, codes[:, None], 0), axis=0).reshape(n, cap)
    incoming = lax.all_to_all(outgoing, "seq", split_axis=0, concat_axis=0, tiled=True)
    wanted = incoming.reshape(n * cap)

    forward = [(i, (i + 1) % n) for i in range(n)]
    backward = [(t, s) for s, t in forward]
    low = lax.ppermute(jnp.stack([keys[-block_len:], values[-block_len:]]), "seq", forward)
    high = lax.ppermute(jnp.stack([keys[:block_len], values[:block_len]]), "seq", backward)

    holders = global_blocks // block_count
    offsets = global_blocks % block_count * block_len
    share = n // g
    thin = block_len * width // (share * head_dim)

    def cut(array, member):
        piece = lax.dynamic_slice_in_dim(array, offsets[member], block_len, 0)
        return piece.reshape(share, thin // 2, wide)

    pieces = jnp.concatenate(
        [jnp.concatenate([cut(keys, m), cut(values, m)], axis=1) for m in range(g)], axis=0
    )
    packed = pack(wanted, keys, values, pieces, cap, block_len, head_dim, head_count)
    arrived = lax.all_to_all(packed, "seq", split_axis=0, concat_axis=0, tiled=True)
    source = holders[lax.axis_index("seq") // share]
    mine = lax.dynamic_slice(arrived, (source, cap * block_len, 0), (1, thin, wide))
    shared = lax.all_gather(mine, "seq", axis=0, tiled=True)
    kg = shared[:, : thin // 2].reshape(g * block_len, width)
    vg = shared[:, thin // 2 :].reshape(g * block_len, width)

    attended = attend(
        owners, ranks, queries, keys, values, low, high, kg, vg, arrived,
        block_count, block_len, head_dim, head_count,
    )
    partial_value = jnp.dot(attended, group_rows, preferred_element_type=f32)
    return lax.psum_scatter(
        partial_value.astype(jnp.bfloat16), "head", scatter_dimension=0, tiled=True
    )


def solution(mesh):
    placed = (
        P("seq", "head"),
        P("seq", "head"),
        P("seq", "head"),
        P("seq", "head"),
        P(),
        P(("head", "seq"), None),
    )
    return jax.shard_map(
        body, mesh=mesh, in_specs=placed, out_specs=P(("seq", "head"), None), check_vma=False
    )
```

```python
import functools

import jax
import jax.numpy as jnp
from jax import lax
from jax.experimental import pallas as pl
from jax.experimental.pallas import tpu as pltpu
from jax.sharding import PartitionSpec as P


def ranked(owners):
    count = owners.shape[0]
    order = jnp.arange(count, dtype=jnp.int32)
    earlier = (owners[:, None] == owners[None, :]) & (order[None, :] < order[:, None])
    return jnp.sum(earlier.astype(jnp.int32), axis=1)


def pack_kernel(cap, block_len, head_dim, head_count, codes_ref, k_ref, v_ref, o_ref):
    dst = pl.program_id(0)
    for s in range(cap):
        code = codes_ref[dst * cap + s]
        row = pl.multiple_of(code // head_count * block_len, block_len)
        col = pl.multiple_of(code % head_count * head_dim, head_dim)
        rows = pl.ds(s * block_len, block_len)
        o_ref[0, rows, 0:head_dim] = k_ref[pl.ds(row, block_len), pl.ds(col, head_dim)]
        o_ref[0, rows, head_dim : 2 * head_dim] = v_ref[pl.ds(row, block_len), pl.ds(col, head_dim)]


def pack(codes, keys, values, n, cap, block_len, head_dim, head_count):
    rows, width = cap * block_len, 2 * head_dim
    whole = lambda d, c: (0, 0)
    return pl.pallas_call(
        functools.partial(pack_kernel, cap, block_len, head_dim, head_count),
        out_shape=jax.ShapeDtypeStruct((n, rows, width), keys.dtype),
        grid_spec=pltpu.PrefetchScalarGridSpec(
            num_scalar_prefetch=1,
            grid=(n,),
            in_specs=[
                pl.BlockSpec(keys.shape, whole),
                pl.BlockSpec(values.shape, whole),
            ],
            out_specs=pl.BlockSpec((1, rows, width), lambda d, c: (d, 0, 0)),
        ),
        cost_estimate=pl.CostEstimate(
            flops=0, transcendentals=0, bytes_accessed=2 * n * rows * width * 2
        ),
        name="pack",
    )(codes, keys, values)


def attend_kernel(
    blocks, block_len, head_dim, head_count, scale,
    own_ref, rank_ref, q_ref, k_ref, v_ref, low_ref, high_ref, kg_ref, vg_ref, arr_ref, o_ref,
):
    h = pl.program_id(0)
    kk = jnp.concatenate([low_ref[0], k_ref[...], high_ref[0]], axis=0)
    vv = jnp.concatenate([low_ref[1], v_ref[...], high_ref[1]], axis=0)
    kg, vg = kg_ref[...], vg_ref[...]
    for b in range(blocks):
        e = b * head_count + h
        owner = own_ref[e]
        rows = pl.ds(pl.multiple_of(rank_ref[e] * block_len, block_len), block_len)
        kr = arr_ref[owner, rows, 0:head_dim]
        vr = arr_ref[owner, rows, head_dim : 2 * head_dim]
        lo, hi = b * block_len, (b + 3) * block_len
        ks = jnp.concatenate([kk[lo:hi], kg, kr], axis=0)
        vs = jnp.concatenate([vv[lo:hi], vg, vr], axis=0)
        q = q_ref[lo : lo + block_len, :]
        s = lax.dot_general(
            q, ks, (((1,), (1,)), ((), ())), preferred_element_type=jnp.float32
        ) * scale
        top = jnp.max(s, axis=-1, keepdims=True)
        expo = jnp.exp(s - top)
        total = jnp.sum(expo, axis=-1, keepdims=True)
        w = (expo * (1.0 / total)).astype(jnp.bfloat16)
        o = jnp.dot(w, vs, preferred_element_type=jnp.float32)
        o_ref[lo : lo + block_len, :] = o.astype(o_ref.dtype)


def attend(owners, ranks, q, k, v, low, high, kg, vg, arrived, blocks, block_len, head_dim, head_count):
    tokens, width = q.shape
    col = lambda h, a, b: (0, h)
    edge = pl.BlockSpec((2, block_len, head_dim), lambda h, a, b: (0, 0, h))
    main = pl.BlockSpec((tokens, head_dim), col)
    glob = pl.BlockSpec((kg.shape[0], head_dim), col)
    return pl.pallas_call(
        functools.partial(
            attend_kernel, blocks, block_len, head_dim, head_count, head_dim ** (-0.5)
        ),
        out_shape=jax.ShapeDtypeStruct(q.shape, jnp.bfloat16),
        grid_spec=pltpu.PrefetchScalarGridSpec(
            num_scalar_prefetch=2,
            grid=(head_count,),
            in_specs=[
                main, main, main, edge, edge, glob, glob,
                pl.BlockSpec(arrived.shape, lambda h, a, b: (0, 0, 0)),
            ],
            out_specs=main,
        ),
        cost_estimate=pl.CostEstimate(
            flops=4 * tokens * 6 * block_len * width,
            transcendentals=tokens * 6 * block_len * head_count,
            bytes_accessed=2 * (4 * q.size + arrived.size),
        ),
        name="attend",
    )(owners, ranks, q, k, v, low, high, kg, vg, arrived)


MESH = pl.DeviceIdType.MESH


def exchange_kernel(
    n, source_ref, w_ref, piece_ref, first_ref, last_ref, full_ref, shared_ref, low_ref, high_ref,
    landed, chosen, line_send, line_recv, near_send, near_recv, far_send, far_recv,
    cut_send, cut_recv, give_send, give_recv, edge_send, edge_recv, local,
):
    lines = n // 4
    me = lax.axis_index("seq")
    z, y, x = me // 4, me // 2 % 2, me % 2
    other_y = z * 4 + (1 - y) * 2 + x
    other_x = z * 4 + y * 2 + 1 - x
    half = w_ref.shape[1] // 2

    barrier = pltpu.get_barrier_semaphore()
    for k in range(1, n):
        pl.semaphore_signal(
            barrier, inc=1, device_id={"seq": lax.rem(me + k, n)}, device_id_type=MESH
        )
    pl.semaphore_wait(barrier, n - 1)

    def remote(src, dst, send, recv, target):
        return pltpu.make_async_remote_copy(
            src_ref=src, dst_ref=dst, send_sem=send, recv_sem=recv,
            device_id={"seq": target}, device_id_type=MESH,
        )

    def origin(side, t):
        return (z - t if side == 0 else z + t) * 4

    def exists(side, t):
        return z - t >= 0 if side == 0 else z + t < lines

    def held(side, t):
        return w_ref if t == 0 else full_ref.at[origin(side, t) + y * 2 + x]

    def along(side, t):
        target = me + 4 if side == 0 else me - 4
        index = origin(side, t) + y * 2 + x
        return remote(
            held(side, t), full_ref.at[index], line_send.at[side, t], line_recv.at[side, t], target
        )

    def passes(side, t):
        ahead = z + 1 < lines if side == 0 else z >= 1
        return jnp.logical_and(exists(side, t), ahead)

    def near(side, t, way):
        index = origin(side, t) + y * 2 + x
        return remote(
            held(side, t), full_ref.at[index], near_send.at[side, t, way],
            near_recv.at[side, t, way], other_y if way == 0 else other_x,
        )

    def far(side, t, way):
        index = origin(side, t) + (
            (1 - y) * 2 + x if way == 0 else y * 2 + 1 - x
        )
        cols = pl.ds(way * half, half)
        return remote(
            full_ref.at[index, :, cols], full_ref.at[index, :, cols], far_send.at[side, t, way],
            far_recv.at[side, t, way], other_x if way == 0 else other_y,
        )

    def sides(t):
        return (0,) if t == 0 else (0, 1)

    def advance(t):
        for side in (0, 1):
            if t > 0:
                @pl.when(exists(side, t))
                def _():
                    along(side, t - 1).wait_recv()
            if t < lines - 1:
                @pl.when(passes(side, t))
                def _():
                    along(side, t).start()
        for side in sides(t):
            @pl.when(exists(side, t))
            def _():
                near(side, t, 0).start()
                near(side, t, 1).start()

    def forward(t):
        for side in sides(t):
            @pl.when(exists(side, t))
            def _():
                for way in (0, 1):
                    near(side, t, way).wait_recv()
                    far(side, t, way).start()

    def cut(k):
        target = lax.rem(me + k, n)
        return remote(
            piece_ref.at[target], landed.at[me], cut_send.at[k], cut_recv.at[k], target
        )

    def give(k):
        target = lax.rem(me + k, n)
        return remote(chosen, shared_ref.at[me], give_send.at[k], give_recv.at[k], target)

    low = remote(last_ref, low_ref, edge_send.at[0], edge_recv.at[0], lax.rem(me + 1, n))
    high = remote(first_ref, high_ref, edge_send.at[1], edge_recv.at[1], lax.rem(me + n - 1, n))
    own_cut = pltpu.make_async_copy(piece_ref.at[me], landed.at[me], local.at[0])
    own_rows = pltpu.make_async_copy(w_ref, full_ref.at[me], local.at[1])
    own_give = pltpu.make_async_copy(chosen, shared_ref.at[me], local.at[2])

    for k in range(1, n):
        cut(k).start()
    own_cut.start()
    own_rows.start()
    advance(0)
    low.start()
    high.start()
    for k in range(1, n):
        cut(k).wait_recv()
    own_cut.wait()
    chosen[...] = landed[source_ref[0]]
    for t in range(1, lines):
        advance(t)
        if t == 1:
            for k in range(1, n):
                give(k).start()
            own_give.start()
        forward(t - 1)
    forward(lines - 1)

    for t in range(lines):
        for side in (0, 1):
            if t < lines - 1:
                @pl.when(passes(side, t))
                def _():
                    along(side, t).wait_send()
        for side in sides(t):
            @pl.when(exists(side, t))
            def _():
                for way in (0, 1):
                    near(side, t, way).wait_send()
                    far(side, t, way).wait()
    for k in range(1, n):
        cut(k).wait_send()
        give(k).wait()
    own_give.wait()
    own_rows.wait()
    low.wait()
    high.wait()


def exchange(source, weight, pieces, first, last, n):
    lines = n // 4
    rows, columns = weight.shape
    dma = pltpu.SemaphoreType.DMA
    vmem = pl.BlockSpec(memory_space=pltpu.VMEM)
    hbm = pl.BlockSpec(memory_space=pl.ANY)
    kind = weight.dtype
    return pl.pallas_call(
        functools.partial(exchange_kernel, n),
        out_shape=(
            jax.ShapeDtypeStruct((n, rows, columns), kind),
            jax.ShapeDtypeStruct(pieces.shape, kind),
            jax.ShapeDtypeStruct(first.shape, kind),
            jax.ShapeDtypeStruct(first.shape, kind),
        ),
        in_specs=[pl.BlockSpec(memory_space=pltpu.SMEM), vmem, vmem, vmem, vmem],
        out_specs=(hbm, hbm, hbm, hbm),
        scratch_shapes=[
            pltpu.VMEM(pieces.shape, kind),
            pltpu.VMEM(pieces.shape[1:], kind),
            dma((2, lines)), dma((2, lines)),
            dma((2, lines, 2)), dma((2, lines, 2)),
            dma((2, lines, 2)), dma((2, lines, 2)),
            dma((n,)), dma((n,)), dma((n,)), dma((n,)),
            dma((2,)), dma((2,)), dma((3,)),
        ],
        compiler_params=pltpu.CompilerParams(collective_id=0, has_side_effects=True),
        cost_estimate=pl.CostEstimate(
            flops=0, transcendentals=0, bytes_accessed=40 * n * rows * columns
        ),
        name="exchange",
    )(source, weight, pieces, first, last)


def body(queries, keys, values, rand_blocks, global_blocks, out_weight):
    f32 = jnp.float32
    n = lax.axis_size("seq")
    block_count, head_count = rand_blocks.shape
    tokens, width = queries.shape
    block_len = tokens // block_count
    head_dim = width // head_count
    entries = block_count * head_count
    cap = max(2, (2 * entries + n - 1) // n)
    g = global_blocks.shape[0]
    wide = 2 * head_dim

    flat_blocks = rand_blocks.reshape(entries)
    owners = flat_blocks // block_count
    head_iota = jnp.arange(entries, dtype=jnp.int32) % head_count
    codes = flat_blocks % block_count * head_count + head_iota
    ranks = ranked(owners)
    slots = owners * cap + ranks
    hits = slots[:, None] == jnp.arange(n * cap, dtype=jnp.int32)[None, :]
    outgoing = jnp.sum(jnp.where(hits, codes[:, None], 0), axis=0).reshape(n, cap)
    incoming = lax.all_to_all(outgoing, "seq", split_axis=0, concat_axis=0, tiled=True)
    wanted = incoming.reshape(n * cap)

    holders = global_blocks // block_count
    offsets = global_blocks % block_count * block_len
    share = n // g
    thin = block_len * width // (share * head_dim)

    def cut(array, member):
        piece = lax.dynamic_slice_in_dim(array, offsets[member], block_len, 0)
        return piece.reshape(share, thin // 2, wide)

    pieces = jnp.concatenate(
        [jnp.concatenate([cut(keys, m), cut(values, m)], axis=1) for m in range(g)], axis=0
    )
    packed = pack(wanted, keys, values, n, cap, block_len, head_dim, head_count)
    arrived = lax.all_to_all(packed, "seq", split_axis=0, concat_axis=0, tiled=True)
    source = holders[lax.axis_index("seq") // share].reshape(1)
    first = jnp.stack([keys[:block_len], values[:block_len]])
    last = jnp.stack([keys[-block_len:], values[-block_len:]])
    weight, packed = lax.optimization_barrier((out_weight, packed))
    group_rows, shared, low, high = exchange(source, weight, pieces, first, last, n)
    group_rows = group_rows.reshape(n * out_weight.shape[0], out_weight.shape[1])
    kg = shared[:, : thin // 2].reshape(g * block_len, width)
    vg = shared[:, thin // 2 :].reshape(g * block_len, width)

    attended = attend(
        owners, ranks, queries, keys, values, low, high, kg, vg, arrived,
        block_count, block_len, head_dim, head_count,
    )
    partial_value = jnp.dot(attended, group_rows, preferred_element_type=f32)
    return lax.psum_scatter(
        partial_value.astype(jnp.bfloat16), "head", scatter_dimension=0, tiled=True
    )


def solution(mesh):
    placed = (
        P("seq", "head"),
        P("seq", "head"),
        P("seq", "head"),
        P("seq", "head"),
        P(),
        P(("head", "seq"), None),
    )
    return jax.shard_map(
        body, mesh=mesh, in_specs=placed, out_specs=P(("seq", "head"), None), check_vma=False
    )
```
